512 devices in a mesh: gx: 32 (over z_lo, y), gy: 16 (over z_hi, x, core).
Axes of the slice: x: 4, y: 4, z: 16 (z_hi: 2, z_lo: 8; z = z_hi * 8 + z_lo), core: 2. Of those that a mesh axis runs over, the one named last changes fastest.
Arguments:
- coeffs: bfloat16 [18, 8, 256, 4096], P(None, None, 'gx', 'gy'), may hold values from 0.5 to 1.5
- sigma: float32 [8, 256, 4096], P(None, 'gx', 'gy'), may hold values from 0.5 to 2
- rhs: float32 [8, 256, 4096], P(None, 'gx', 'gy'), may hold values from -48 to 48
- vel_bar: bfloat16 [3, 8, 256, 4096], P(None, None, 'gx', 'gy'), may hold values from -6 to 6
- metric: bfloat16 [3, 8, 256, 4096], P(None, None, 'gx', 'gy'), may hold values from 0.5 to 2
Outputs:
- pressure_adj: float32 [8, 256, 4096], P(None, 'gx', 'gy')
- vel_out: float32 [3, 8, 256, 4096], P(None, None, 'gx', 'gy')
The draws below stay inside these ranges and needn't reach their ends.
All inputs are finite; a program needn't handle non-finite values.
Results may differ from the reference program's by a relative error of at most 0.0003.
Values may be sent and summed in bfloat16 or wider, within the bound.
A program may use at most 64 MiB of HBM per device.

```python
import math
import jax
import jax.numpy as jnp

NZ = 8
SWEEPS = 6
NX = 256
NY = 4096


def draw_rhs(key, part):
    rough = 8.0 * jax.random.normal(key, (NZ, NX, NY), jnp.float32)
    return jnp.clip(rough, -48.0, 48.0)


def shard_levels(rng, dims, split, smallest, top_value):
    def one(dim, parts):
        steps = jax.random.uniform(jax.random.fold_in(jax.random.fold_in(rng, 6), dim), (parts,), jnp.float32, smallest / len(split), top_value / len(split))
        return jnp.repeat(jnp.exp(steps), dims[dim] // parts).reshape((-1,) + (1,) * (len(dims) - dim - 1))

    factor_of = one(*split[0])
    for cut in split[1:]:
        factor_of = factor_of * one(*cut)
    return factor_of


def gaussian(rng, dims, scale, most, cuts=(), kind=jnp.bfloat16):
    array = jax.random.normal(rng, dims, jnp.float32) * scale
    if len(cuts) > 0:
        array = shard_levels(rng, dims, cuts, -0.22, 0.18) * array
    return jnp.clip(array, min=-most, max=most).astype(kind)


def setup_inputs(seed: int = 0) -> dict:
    streams_of = jax.random.split(jax.random.key(seed), 6)
    coeffs = jnp.clip(0.5 + 1.0 * jax.random.uniform(streams_of[0], (18, NZ, NX, NY), jnp.float32) ** shard_levels(streams_of[0], (18, NZ, NX, NY), ((2, 32), (3, 16)), -0.2, 0.2), 0.5, 1.5).astype(jnp.bfloat16)
    sigma = jnp.clip(jnp.exp(math.log(2.0) - 1.3862944 * jax.random.uniform(streams_of[1], (NZ, NX, NY), jnp.float32) ** shard_levels(streams_of[1], (NZ, NX, NY), ((1, 32), (2, 16)), -0.2, 0.2)), 0.5, 2.0)
    rhs = draw_rhs(jax.random.fold_in(streams_of[5], 71), 0)
    vel_bar = gaussian(streams_of[3], (3, NZ, NX, NY), 1.0, 6.0, ((2, 32), (3, 16)))
    metric = jnp.clip(jnp.exp(math.log(2.0) - 1.3862944 * jax.random.uniform(streams_of[4], (3, NZ, NX, NY), jnp.float32) ** shard_levels(streams_of[4], (3, NZ, NX, NY), ((2, 32), (3, 16)), -0.2, 0.2)), 0.5, 2.0).astype(jnp.bfloat16)
    return {"coeffs": coeffs, "sigma": sigma, "rhs": rhs, "vel_bar": vel_bar, "metric": metric}


OFFSETS = ((1, 0, 0), (-1, 0, 0), (0, 1, 0), (0, -1, 0), (0, 0, 1), (0, 0, -1),
           (0, 1, 1), (0, 1, -1), (0, -1, 1), (0, -1, -1),
           (1, 1, 0), (1, -1, 0), (-1, 1, 0), (-1, -1, 0),
           (1, 0, 1), (1, 0, -1), (-1, 0, 1), (-1, 0, -1))
WEIGHTS = (1.0,) * 6 + (0.25,) * 12


def shift_levels(field, step):
    if step == 0:
        return field
    zero = jnp.zeros_like(field[:1])
    if step == 1:
        return jnp.concatenate([zero, field[:-1]], axis=0)
    return jnp.concatenate([field[1:], zero], axis=0)


def apply_transpose(field, coeffs, diag):
    total = diag * field
    for index in range(18):
        step_z, step_x, step_y = OFFSETS[index]
        product = WEIGHTS[index] * coeffs[index].astype(jnp.float32) * field
        moved = jnp.roll(product, (step_x, step_y), axis=(1, 2))
        total = total - shift_levels(moved, step_z)
    return total


def reference(coeffs, sigma, rhs, vel_bar, metric):
    diag = sigma
    for index in range(18):
        diag = diag + WEIGHTS[index] * coeffs[index].astype(jnp.float32)
    lmin, lmax = 0.5, 31.0
    theta = (lmax + lmin) / 2.0
    delta = (lmax - lmin) / 2.0
    s_one = theta / delta
    rho = 1.0 / s_one
    pressure = jnp.zeros_like(rhs)
    residue = rhs
    direction = rhs / theta
    for sweep in range(SWEEPS):
        pressure = pressure + direction
        residue = residue - apply_transpose(direction, coeffs, diag)
        rho_new = 1.0 / (2.0 * s_one - rho)
        direction = rho_new * rho * direction + (2.0 * rho_new / delta) * residue
        rho = rho_new
    grad_x = (jnp.roll(pressure, -1, axis=1) - jnp.roll(pressure, 1, axis=1)) * 0.5
    grad_y = (jnp.roll(pressure, -1, axis=2) - jnp.roll(pressure, 1, axis=2)) * 0.5
    grad_z = (shift_levels(pressure, -1) - shift_levels(pressure, 1)) * 0.5
    grads = jnp.stack([grad_x, grad_y, grad_z])
    vel_out = vel_bar.astype(jnp.float32) - metric.astype(jnp.float32) * grads
    return pressure, vel_out
```

```python
import functools

import jax
import jax.numpy as jnp
from jax import lax
from jax.experimental import pallas as pl
from jax.experimental.pallas import tpu as pltpu
from jax.sharding import PartitionSpec as P

SWEEPS = 6
APPLIES = SWEEPS - 1
HALO = APPLIES + 1
LMIN, LMAX = 0.5, 31.0
LANES = 128

OFFSETS = (
    (1, 0, 0),
    (-1, 0, 0),
    (0, 1, 0),
    (0, -1, 0),
    (0, 0, 1),
    (0, 0, -1),
    (0, 1, 1),
    (0, 1, -1),
    (0, -1, 1),
    (0, -1, -1),
    (1, 1, 0),
    (1, -1, 0),
    (-1, 1, 0),
    (-1, -1, 0),
    (1, 0, 1),
    (1, 0, -1),
    (-1, 0, 1),
    (-1, 0, -1),
)
WEIGHTS = (1.0,) * 6 + (0.25,) * 12
TERMS = len(OFFSETS)
SIGMA, RHS_HIGH, RHS_LOW = TERMS, TERMS + 1, TERMS + 2
SENT = TERMS + 3
INDEX = {offset: i for i, offset in enumerate(OFFSETS)}
SIDES = ((-1, -1), (-1, 1), (1, -1), (1, 1), (0, -1), (0, 1), (-1, 0), (1, 0))


def roll(value, shift, axis):
    size = value.shape[axis]
    return pltpu.roll(value, shift % size, axis)


def kernel(
    count_x,
    count_y,
    coeffs_ref,
    sigma_ref,
    rhs_ref,
    pressure_ref,
    grads_ref,
    sent,
    packed_low,
    packed_high,
    from_high,
    from_low,
    terms,
    diag,
    turn,
    direction,
    residue,
    pressure,
    send_sem,
    recv_sem,
):
    levels, cells_x, cells_y = rhs_ref.shape
    rows = cells_x + 2 * HALO
    me_x, me_y = lax.axis_index("gx"), lax.axis_index("gy")

    def device(side):
        return (
            lax.rem(me_x + side[0] + count_x, count_x),
            lax.rem(me_y + side[1] + count_y, count_y),
        )

    barrier = pltpu.get_barrier_semaphore()
    for side in SIDES:
        pl.semaphore_signal(
            barrier, inc=1, device_id=device(side), device_id_type=pl.DeviceIdType.MESH
        )

    level = lax.broadcasted_iota(jnp.int32, (levels, cells_y), 0)

    tiles = cells_y // LANES

    def turned(value):
        value = value.reshape(levels * cells_x, cells_y)
        for t in range(tiles):
            turn[t] = value[:, t * LANES : (t + 1) * LANES]
        return [
            jnp.concatenate(
                [turn[t, pl.ds(x, levels, stride=cells_x), :] for t in range(tiles)], axis=1
            )
            for x in range(cells_x)
        ]

    sigma_rows = turned(sigma_ref[...])
    for x in range(cells_x):
        diag[HALO + x, :, :cells_y] = sigma_rows[x]
        residue[x, :, :cells_y] = sigma_rows[x]
    for i in range(TERMS):
        step_z = OFFSETS[i][0]
        for x, value in enumerate(turned(coeffs_ref[i].astype(jnp.float32) * WEIGHTS[i])):
            row = HALO + x
            diag[row, :, :cells_y] = diag[row, :, :cells_y] + value
            if step_z != 0:
                leaves = level == (levels - 1 if step_z == 1 else 0)
                residue[x, :, :cells_y] = residue[x, :, :cells_y] + jnp.where(leaves, value, 0.0)
                value = jnp.where(leaves, 0.0, value)
            terms[row, i, :, :cells_y] = value
            sent[row, i, :, :cells_y] = value.astype(jnp.bfloat16)
    for x in range(cells_x):
        sent[HALO + x, SIGMA, :, :cells_y] = residue[x, :, :cells_y].astype(jnp.bfloat16)
    for x, value in enumerate(turned(rhs_ref[...])):
        row = HALO + x
        residue[row, :, :cells_y] = value
        high = value.astype(jnp.bfloat16)
        sent[row, RHS_HIGH, :, :cells_y] = high
        sent[row, RHS_LOW, :, :cells_y] = (value - high.astype(jnp.float32)).astype(jnp.bfloat16)

    lane = lax.broadcasted_iota(jnp.int32, (levels, LANES), 1)

    def pack(x, carry):
        low = jnp.zeros((levels, LANES), jnp.float32)
        high = jnp.zeros((levels, LANES), jnp.float32)
        for i in range(SENT):
            here = (lane >= HALO * i) & (lane < HALO * (i + 1))
            first = sent[HALO + x, i, :, :LANES].astype(jnp.float32)
            last = sent[HALO + x, i, :, cells_y - LANES : cells_y].astype(jnp.float32)
            low = jnp.where(here, roll(first, HALO * i, 1), low)
            high = jnp.where(here, roll(last, HALO * i + HALO, 1), high)
        packed_low[x] = low.astype(jnp.bfloat16)
        packed_high[x] = high.astype(jnp.bfloat16)
        return carry

    lax.fori_loop(0, cells_x, pack, 0)

    pl.semaphore_wait(barrier, len(SIDES))

    copies = []
    for n, (dx, dy) in enumerate(SIDES):
        first, there = {-1: (0, HALO + cells_x), 0: (0, HALO), 1: (cells_x - HALO, 0)}[dx]
        count = cells_x if dx == 0 else HALO
        if dy == 0:
            source = sent.at[pl.ds(HALO + first, count), :, :, pl.ds(0, cells_y)]
            target = sent.at[pl.ds(there, count), :, :, pl.ds(0, cells_y)]
        elif dy == -1:
            source = packed_low.at[pl.ds(first, count)]
            target = from_high.at[pl.ds(there, count)]
        else:
            source = packed_high.at[pl.ds(first, count)]
            target = from_low.at[pl.ds(there, count)]
        copy = pltpu.make_async_remote_copy(
            src_ref=source,
            dst_ref=target,
            send_sem=send_sem.at[n],
            recv_sem=recv_sem.at[n],
            device_id=device((dx, dy)),
            device_id_type=pl.DeviceIdType.MESH,
        )
        copy.start()
        copies.append(copy)
    for copy in copies:
        copy.wait()

    def spread(first):
        def body(step, carry):
            row = first + step
            total = sent[row, SIGMA, :, :cells_y].astype(jnp.float32)
            for i in range(TERMS):
                value = sent[row, i, :, :cells_y].astype(jnp.float32)
                terms[row, i, :, :cells_y] = value
                total = total + value
            diag[row, :, :cells_y] = total
            residue[row, :, :cells_y] = sent[row, RHS_HIGH, :, :cells_y].astype(
                jnp.float32
            ) + sent[row, RHS_LOW, :, :cells_y].astype(jnp.float32)
            return carry

        lax.fori_loop(0, HALO, body, 0)

    spread(0)
    spread(HALO + cells_x)

    def unpack(row, carry):
        above = from_high[row].astype(jnp.float32)
        below = from_low[row].astype(jnp.float32)

        def field(i):
            return jnp.where(
                lane < LANES // 2,
                roll(above, -HALO * i, 1),
                roll(below, LANES - HALO - HALO * i, 1),
            )

        total = field(SIGMA)
        for i in range(TERMS):
            value = field(i)
            terms[row, i, :, cells_y:] = value
            total = total + value
        diag[row, :, cells_y:] = total
        residue[row, :, cells_y:] = field(RHS_HIGH) + field(RHS_LOW)
        return carry

    lax.fori_loop(0, rows, unpack, 0)

    theta = (LMAX + LMIN) / 2.0
    delta = (LMAX - LMIN) / 2.0
    s_one = theta / delta
    rho = 1.0 / s_one

    def begin(row, carry):
        value = residue[row] / theta
        direction[0, row] = value
        pressure[row] = value
        return carry

    lax.fori_loop(0, rows, begin, 0)

    for sweep in range(1, APPLIES + 1):
        rho_new = 1.0 / (2.0 * s_one - rho)
        now, later = (sweep - 1) % 2, sweep % 2

        def apply(row, carry, now=now, later=later, rho=rho, rho_new=rho_new):
            field = {step: direction[now, row - step] for step in (-1, 0, 1)}

            def along(step_z, step_y):
                total = None
                for step_x in (-1, 0, 1):
                    i = INDEX.get((step_z, step_x, step_y))
                    if i is not None:
                        term = terms[row - step_x, i] * field[step_x]
                        total = term if total is None else total + term
                return total

            def levels_moved(step_y):
                return roll(along(1, step_y), 1, 0) + roll(along(-1, step_y), -1, 0)

            total = along(0, 0) + levels_moved(0)
            total = total + roll(along(0, 1) + levels_moved(1), 1, 1)
            total = total + roll(along(0, -1) + levels_moved(-1), -1, 1)
            left = residue[row] - (diag[row] * field[0] - total)
            residue[row] = left
            value = rho_new * rho * field[0] + 2.0 * rho_new / delta * left
            direction[later, row] = value
            pressure[row] = pressure[row] + value
            return carry

        lax.fori_loop(sweep, rows - sweep, apply, 0)
        rho = rho_new

    level = lax.broadcasted_iota(jnp.int32, (levels, pressure.shape[2]), 0)

    def gradient(x, carry):
        row = HALO + x
        here = pressure[row]
        grad_x = (pressure[row + 1] - pressure[row - 1]) * 0.5
        grad_y = (roll(here, -1, 1) - roll(here, 1, 1)) * 0.5
        upper = jnp.where(level == levels - 1, 0.0, roll(here, -1, 0))
        lower = jnp.where(level == 0, 0.0, roll(here, 1, 0))
        grad_z = (upper - lower) * 0.5
        pressure_ref[x] = here[:, :cells_y]
        for n, grad in enumerate((grad_x, grad_y, grad_z)):
            grads_ref[n, x] = grad[:, :cells_y]
        return carry

    lax.fori_loop(0, cells_x, gradient, 0)


def on_device(count_x, count_y, coeffs, sigma, rhs, vel_bar, metric):
    levels, cells_x, cells_y = rhs.shape
    rows, width = cells_x + 2 * HALO, cells_y + LANES
    vmem = pl.BlockSpec(memory_space=pltpu.VMEM)
    pressure, grads = pl.pallas_call(
        functools.partial(kernel, count_x, count_y),
        out_shape=(
            jax.ShapeDtypeStruct((cells_x, levels, cells_y), jnp.float32),
            jax.ShapeDtypeStruct((3, cells_x, levels, cells_y), jnp.float32),
        ),
        in_specs=[vmem] * 3,
        out_specs=(vmem, vmem),
        scratch_shapes=[
            pltpu.VMEM((rows, SENT, levels, width), jnp.bfloat16),
            pltpu.VMEM((cells_x, levels, LANES), jnp.bfloat16),
            pltpu.VMEM((cells_x, levels, LANES), jnp.bfloat16),
            pltpu.VMEM((rows, levels, LANES), jnp.bfloat16),
            pltpu.VMEM((rows, levels, LANES), jnp.bfloat16),
            pltpu.VMEM((rows, TERMS, levels, width), jnp.float32),
            pltpu.VMEM((rows, levels, width), jnp.float32),
            pltpu.VMEM((cells_y // LANES, levels * cells_x, LANES), jnp.float32),
            pltpu.VMEM((2, rows, levels, width), jnp.float32),
            pltpu.VMEM((rows, levels, width), jnp.float32),
            pltpu.VMEM((rows, levels, width), jnp.float32),
            pltpu.SemaphoreType.DMA((len(SIDES),)),
            pltpu.SemaphoreType.DMA((len(SIDES),)),
        ],
        compiler_params=pltpu.CompilerParams(collective_id=0, has_side_effects=True),
    )(coeffs, sigma, rhs)
    pressure = jnp.transpose(pressure, (1, 0, 2))
    grads = jnp.transpose(grads, (0, 2, 1, 3))
    vel_out = vel_bar.astype(jnp.float32) - metric.astype(jnp.float32) * grads
    return (pressure, vel_out)


def solution(mesh):
    return jax.shard_map(
        functools.partial(on_device, mesh.shape["gx"], mesh.shape["gy"]),
        mesh=mesh,
        in_specs=(
            P(None, None, "gx", "gy"),
            P(None, "gx", "gy"),
            P(None, "gx", "gy"),
            P(None, None, "gx", "gy"),
            P(None, None, "gx", "gy"),
        ),
        out_specs=(P(None, "gx", "gy"), P(None, None, "gx", "gy")),
        check_vma=False,
    )
```

```python
import functools

import jax
import jax.numpy as jnp
from jax import lax
from jax.experimental import pallas as pl
from jax.experimental.pallas import tpu as pltpu
from jax.sharding import PartitionSpec as P

SWEEPS = 6
APPLIES = SWEEPS - 1
HALO = APPLIES + 1
LMIN, LMAX = 0.5, 31.0
LANES = 128
TOGETHER = 2

OFFSETS = (
    (1, 0, 0),
    (-1, 0, 0),
    (0, 1, 0),
    (0, -1, 0),
    (0, 0, 1),
    (0, 0, -1),
    (0, 1, 1),
    (0, 1, -1),
    (0, -1, 1),
    (0, -1, -1),
    (1, 1, 0),
    (1, -1, 0),
    (-1, 1, 0),
    (-1, -1, 0),
    (1, 0, 1),
    (1, 0, -1),
    (-1, 0, 1),
    (-1, 0, -1),
)
WEIGHTS = (1.0,) * 6 + (0.25,) * 12
TERMS = len(OFFSETS)
ORDER = (
    [i for i in range(TERMS) if OFFSETS[i][1] == 1]
    + [-1, -2]
    + [i for i in range(TERMS) if OFFSETS[i][1] == -1]
    + [i for i in range(TERMS) if OFFSETS[i][1] == 0]
    + [-3]
)
SENT = len(ORDER)
RHS_HIGH, RHS_LOW, SIGMA = ORDER.index(-1), ORDER.index(-2), ORDER.index(-3)
PLACE = {OFFSETS[i]: n for n, i in enumerate(ORDER) if i >= 0}
OUTER = RHS_LOW + 1
SIDES = ((0, -1), (0, 1), (-1, -1), (-1, 1), (1, -1), (1, 1), (-1, 0), (1, 0))


def roll(value, shift, axis):
    size = value.shape[axis]
    return pltpu.roll(value, shift % size, axis)


def kernel(
    count_x,
    count_y,
    coeffs_ref,
    sigma_ref,
    rhs_ref,
    vel_ref,
    metric_ref,
    pressure_ref,
    out_ref,
    sent,
    packed_low,
    packed_high,
    from_high,
    from_low,
    terms,
    diag,
    turn,
    direction,
    residue,
    pressure,
    send_sem,
    recv_sem,
    outer_send_sem,
    outer_recv_sem,
    token,
):
    levels, cells_x, cells_y = rhs_ref.shape
    rows = cells_x + 2 * HALO
    tiles = cells_y // LANES
    me_x, me_y = lax.axis_index("gx"), lax.axis_index("gy")

    def device(side):
        return (
            lax.rem(me_x + side[0] + count_x, count_x),
            lax.rem(me_y + side[1] + count_y, count_y),
        )

    half = count_y // 2

    def at_seams(x, y):
        y = lax.rem(y, half)
        return ((x == 0) | (x == count_x - 1)) & ((y == 0) | (y == half - 1))

    def over(side):
        over_x = {-1: me_x == 0, 0: me_x < 0, 1: me_x == count_x - 1}[side[0]]
        over_y = {
            -1: lax.rem(me_y, half) == 0,
            0: me_y < 0,
            1: lax.rem(me_y, half) == half - 1,
        }[side[1]]
        return over_x & jnp.logical_not(over_y), over_y & jnp.logical_not(over_x)

    def signal(semaphore, target):
        pl.semaphore_signal(
            semaphore, inc=1, device_id=target, device_id_type=pl.DeviceIdType.MESH
        )

    at_both = at_seams(me_x, me_y)
    inner_y = me_y + 1 - 2 * lax.rem(me_y, 2)
    inner_x = me_x + 1 - 2 * lax.rem(me_x, 2)
    barrier = pltpu.get_barrier_semaphore()
    for side in SIDES:
        target = device(side)
        over_x, over_y = over(side)
        pl.when(jnp.logical_not((over_x | over_y) & at_seams(*target)))(
            functools.partial(signal, barrier, target)
        )

    def turned(value, slot):
        value = value.reshape(levels * cells_x, cells_y)
        for t in range(tiles):
            turn[slot, t] = value[:, t * LANES : (t + 1) * LANES]
        return [
            [turn[slot, t, pl.ds(x, levels, stride=cells_x), :] for t in range(tiles)]
            for x in range(cells_x)
        ]

    def spread(t):
        return slice(t * LANES, (t + 1) * LANES)

    for n, i in enumerate(ORDER):
        if i >= 0:
            value = coeffs_ref[i].astype(jnp.float32) * WEIGHTS[i]
        elif n == SIGMA:
            value = sigma_ref[...]
        elif n == RHS_HIGH:
            value = rhs_ref[...].astype(jnp.bfloat16).astype(jnp.float32)
        else:
            value = rhs_ref[...] - rhs_ref[...].astype(jnp.bfloat16).astype(jnp.float32)
        for x, parts in enumerate(turned(value, n)):
            for t, part in enumerate(parts):
                sent[HALO + x, n, :, spread(t)] = part.astype(jnp.bfloat16)

    lane = lax.broadcasted_iota(jnp.int32, (levels, LANES), 1)

    def pack(x, carry):
        low = jnp.zeros((levels, LANES), jnp.float32)
        high = jnp.zeros((levels, LANES), jnp.float32)
        for n in range(SENT):
            here = (lane >= HALO * n) & (lane < HALO * (n + 1))
            first = sent[HALO + x, n, :, :LANES].astype(jnp.float32)
            last = sent[HALO + x, n, :, cells_y - LANES : cells_y].astype(jnp.float32)
            low = jnp.where(here, roll(first, HALO * n, 1), low)
            high = jnp.where(here, roll(last, HALO * n + HALO, 1), high)
        packed_low[x] = low.astype(jnp.bfloat16)
        packed_high[x] = high.astype(jnp.bfloat16)
        return carry

    lax.fori_loop(0, cells_x, pack, 0)

    pl.semaphore_wait(barrier, jnp.where(at_both, len(SIDES) - 4, len(SIDES)))
    pl.when(at_seams(me_x, inner_y))(lambda: signal(token.at[0], (me_x, inner_y)))
    pl.when(at_seams(inner_x, me_y))(lambda: signal(token.at[1], (inner_x, me_y)))

    copies = []
    for n, side in enumerate(SIDES):
        dx, dy = side
        first, there = {-1: (0, HALO + cells_x), 0: (0, HALO), 1: (cells_x - HALO, 0)}[dx]
        count = cells_x if dx == 0 else HALO
        here = pl.ds(first, count)
        if dy == -1:
            pairs = [(packed_low.at[here], from_high.at[pl.ds(there, count)])]
        elif dy == 1:
            pairs = [(packed_high.at[here], from_low.at[pl.ds(there, count)])]
        else:
            far, fields = (first, pl.ds(0, OUTER)) if dx == 1 else (
                first + count - 1, pl.ds(RHS_HIGH, OUTER))
            skip = 1 if dx == 1 else 0
            width = pl.ds(0, cells_y)
            pairs = [
                (sent.at[pl.ds(HALO + first + k, c), f, :, width], sent.at[pl.ds(there + k, c), f, :, width])
                for k, c, f in (
                    (skip, count - 1, pl.ds(0, SENT)),
                    (far - first, 1, fields),
                )
            ]
        for k, (source, target) in enumerate(pairs):
            copies.append(
                (
                    side,
                    pltpu.make_async_remote_copy(
                        src_ref=source,
                        dst_ref=target,
                        send_sem=(outer_send_sem if k else send_sem).at[n],
                        recv_sem=(outer_recv_sem if k else recv_sem).at[n],
                        device_id=device(side),
                        device_id_type=pl.DeviceIdType.MESH,
                    ),
                )
            )

    for side, copy in copies:
        over_x, over_y = over(side)
        pl.when(jnp.logical_not(at_both & (over_x | over_y)))(copy.start)

    def across(k):
        pl.semaphore_wait(token.at[k], 1)
        for side, copy in copies:
            pl.when(over(side)[k])(copy.start)

    for order, where in (((1, 0), me_x == 0), ((0, 1), me_x != 0)):

        @pl.when(at_both & where)
        def _(order=order):
            for k in order:
                across(k)

    theta = (LMAX + LMIN) / 2.0
    delta = (LMAX - LMIN) / 2.0
    s_one = theta / delta

    def leaves(step_z, shape):
        level = lax.broadcasted_iota(jnp.int32, shape, 0)
        return level == (levels - 1 if step_z == 1 else 0)

    def take(row, at, field, right, wanted):
        total = field(SIGMA) if len(wanted) == SENT else None
        for n in wanted:
            i = ORDER[n]
            if i >= 0:
                value = field(n)
                if total is not None:
                    total = total + value
                if OFFSETS[i][0] != 0:
                    value = jnp.where(leaves(OFFSETS[i][0], value.shape), 0.0, value)
                terms[row, n, :, at] = value
        if total is not None:
            diag[row, :, at] = total
        residue[row, :, at] = right
        direction[0, row, :, at] = right * (1.0 / theta)
        pressure[row, :, at] = right * (1.0 / theta)

    EVERY = range(SENT)
    main, side_lanes = slice(0, cells_y), slice(cells_y, cells_y + LANES)

    for x in range(cells_x):
        row = HALO + x

        def exact(n):
            return jnp.concatenate(
                [turn[n, t, pl.ds(x, levels, stride=cells_x), :] for t in range(tiles)], axis=1
            )

        take(row, main, exact, exact(RHS_HIGH) + exact(RHS_LOW), EVERY)

    def main_field(row):
        return lambda n: sent[row, n, :, :cells_y].astype(jnp.float32)

    def side_field(row):
        above = from_high[row].astype(jnp.float32)
        below = from_low[row].astype(jnp.float32)
        return lambda n: jnp.where(
            lane < LANES // 2,
            roll(above, -HALO * n, 1),
            roll(below, LANES - HALO - HALO * n, 1),
        )

    def receive(make, at, row, wanted=EVERY):
        field = make(row)
        take(row, at, field, field(RHS_HIGH) + field(RHS_LOW), wanted)

    def many(make, at, first, count):
        def body(step, carry):
            receive(make, at, first + step)
            return carry

        lax.fori_loop(0, count, body, 0)

    for side, copy in copies:
        if side[1] != 0:
            copy.wait()
    receive(side_field, side_lanes, 0, range(OUTER))
    many(side_field, side_lanes, 1, rows - 2)
    receive(side_field, side_lanes, rows - 1, range(RHS_HIGH, RHS_HIGH + OUTER))
    for side, copy in copies:
        if side[1] == 0:
            copy.wait()
    receive(main_field, main, 0, range(OUTER))
    many(main_field, main, 1, HALO - 1)
    many(main_field, main, HALO + cells_x, HALO - 1)
    receive(main_field, main, rows - 1, range(RHS_HIGH, RHS_HIGH + OUTER))

    rho = 1.0 / s_one
    for sweep in range(1, APPLIES + 1):
        rho_new = 1.0 / (2.0 * s_one - rho)
        now, later = (sweep - 1) % 2, sweep % 2

        def apply(step, carry, sweep=sweep, now=now, later=later, rho=rho, rho_new=rho_new):
            first = sweep + TOGETHER * step
            fields = [direction[now, first + k - 1] for k in range(TOGETHER + 2)]
            done = []
            for k in range(TOGETHER):
                row = first + k

                def along(step_z, step_y):
                    total = None
                    for step_x in (-1, 0, 1):
                        n = PLACE.get((step_z, step_x, step_y))
                        if n is not None:
                            term = terms[row - step_x, n] * fields[k + 1 - step_x]
                            total = term if total is None else total + term
                    return total

                def levels_moved(step_y):
                    return roll(along(1, step_y), 1, 0) + roll(along(-1, step_y), -1, 0)

                total = along(0, 0) + levels_moved(0)
                total = total + roll(along(0, 1) + levels_moved(1), 1, 1)
                total = total + roll(along(0, -1) + levels_moved(-1), -1, 1)
                left = residue[row] - (diag[row] * fields[k + 1] - total)
                value = rho_new * rho * fields[k + 1] + 2.0 * rho_new / delta * left
                done.append((row, left, value, pressure[row] + value))
            for row, left, value, summed in done:
                residue[row] = left
                direction[later, row] = value
                pressure[row] = summed
            return carry

        lax.fori_loop(0, (rows - 2 * sweep) // TOGETHER, apply, 0)
        rho = rho_new

    shape = pressure.shape[1:]
    for x in range(cells_x):
        row = HALO + x
        here = pressure[row]
        grad_x = (pressure[row + 1] - pressure[row - 1]) * 0.5
        grad_y = (roll(here, -1, 1) - roll(here, 1, 1)) * 0.5
        upper = jnp.where(leaves(1, shape), 0.0, roll(here, -1, 0))
        lower = jnp.where(leaves(-1, shape), 0.0, roll(here, 1, 0))
        grad_z = (upper - lower) * 0.5
        for n, value in enumerate((grad_x, grad_y, grad_z, here)):
            for t in range(tiles):
                turn[n, t, pl.ds(x * levels, levels), :] = value[:, spread(t)]
    for z in range(levels):
        for t in range(tiles):
            at = spread(t)
            back = [turn[n, t, pl.ds(z, cells_x, stride=levels), :] for n in range(4)]
            pressure_ref[z, :, at] = back[3]
            for n in range(3):
                out_ref[n, z, :, at] = (
                    vel_ref[n, z, :, at].astype(jnp.float32)
                    - metric_ref[n, z, :, at].astype(jnp.float32) * back[n]
                )


def on_device(count_x, count_y, coeffs, sigma, rhs, vel_bar, metric):
    levels, cells_x, cells_y = rhs.shape
    rows, width = cells_x + 2 * HALO, cells_y + LANES
    vmem = pl.BlockSpec(memory_space=pltpu.VMEM)
    return pl.pallas_call(
        functools.partial(kernel, count_x, count_y),
        out_shape=(
            jax.ShapeDtypeStruct(rhs.shape, jnp.float32),
            jax.ShapeDtypeStruct(vel_bar.shape, jnp.float32),
        ),
        in_specs=[vmem] * 5,
        out_specs=(vmem, vmem),
        scratch_shapes=[
            pltpu.VMEM((rows, SENT, levels, width), jnp.bfloat16),
            pltpu.VMEM((cells_x, levels, LANES), jnp.bfloat16),
            pltpu.VMEM((cells_x, levels, LANES), jnp.bfloat16),
            pltpu.VMEM((rows, levels, LANES), jnp.bfloat16),
            pltpu.VMEM((rows, levels, LANES), jnp.bfloat16),
            pltpu.VMEM((rows, SENT, levels, width), jnp.float32),
            pltpu.VMEM((rows, levels, width), jnp.float32),
            pltpu.VMEM((SENT, cells_y // LANES, levels * cells_x, LANES), jnp.float32),
            pltpu.VMEM((2, rows, levels, width), jnp.float32),
            pltpu.VMEM((rows, levels, width), jnp.float32),
            pltpu.VMEM((rows, levels, width), jnp.float32),
            pltpu.SemaphoreType.DMA((len(SIDES),)),
            pltpu.SemaphoreType.DMA((len(SIDES),)),
            pltpu.SemaphoreType.DMA((len(SIDES),)),
            pltpu.SemaphoreType.DMA((len(SIDES),)),
            pltpu.SemaphoreType.REGULAR((2,)),
        ],
        compiler_params=pltpu.CompilerParams(collective_id=0, has_side_effects=True),
    )(coeffs, sigma, rhs, vel_bar, metric)


def solution(mesh):
    return jax.shard_map(
        functools.partial(on_device, mesh.shape["gx"], mesh.shape["gy"]),
        mesh=mesh,
        in_specs=(
            P(None, None, "gx", "gy"),
            P(None, "gx", "gy"),
            P(None, "gx", "gy"),
            P(None, None, "gx", "gy"),
            P(None, None, "gx", "gy"),
        ),
        out_specs=(P(None, "gx", "gy"), P(None, None, "gx", "gy")),
        check_vma=False,
    )
```

```python
import functools

import jax
import jax.numpy as jnp
from jax import lax
from jax.experimental import pallas as pl
from jax.experimental.pallas import tpu as pltpu
from jax.sharding import PartitionSpec as P

SWEEPS = 6
APPLIES = SWEEPS - 1
HALO = APPLIES + 1
LMIN, LMAX = 0.5, 31.0
LANES = 128

OFFSETS = (
    (1, 0, 0),
    (-1, 0, 0),
    (0, 1, 0),
    (0, -1, 0),
    (0, 0, 1),
    (0, 0, -1),
    (0, 1, 1),
    (0, 1, -1),
    (0, -1, 1),
    (0, -1, -1),
    (1, 1, 0),
    (1, -1, 0),
    (-1, 1, 0),
    (-1, -1, 0),
    (1, 0, 1),
    (1, 0, -1),
    (-1, 0, 1),
    (-1, 0, -1),
)
WEIGHTS = (1.0,) * 6 + (0.25,) * 12
TERMS = len(OFFSETS)
ORDER = (
    [i for i in range(TERMS) if OFFSETS[i][1] == 1]
    + [-1, -2]
    + [i for i in range(TERMS) if OFFSETS[i][1] == -1]
    + [i for i in range(TERMS) if OFFSETS[i][1] == 0]
    + [-3]
)
SENT = len(ORDER)
RHS_HIGH, RHS_LOW, SIGMA = ORDER.index(-1), ORDER.index(-2), ORDER.index(-3)
PLACE = {OFFSETS[i]: n for n, i in enumerate(ORDER) if i >= 0}
OUTER = RHS_LOW + 1
SIDES = ((0, -1), (0, 1), (-1, -1), (-1, 1), (1, -1), (1, 1), (-1, 0), (1, 0))


def roll(value, shift, axis):
    size = value.shape[axis]
    return pltpu.roll(value, shift % size, axis)


def kernel(
    count_x,
    count_y,
    coeffs_hbm,
    sigma_hbm,
    rhs_hbm,
    pressure_ref,
    coeffs_ref,
    sigma_ref,
    rhs_ref,
    load_sem,
    sent,
    packed_low,
    packed_high,
    from_high,
    from_low,
    terms,
    ends,
    diag,
    turn,
    direction,
    residue,
    pressure,
    send_sem,
    recv_sem,
    row_send_sem,
    row_recv_sem,
    token,
):
    loads = [
        pltpu.make_async_copy(source, target, load_sem.at[n])
        for n, (source, target) in enumerate(
            ((coeffs_hbm, coeffs_ref), (sigma_hbm, sigma_ref), (rhs_hbm, rhs_ref))
        )
    ]
    for load in loads:
        load.start()
    levels, cells_x, cells_y = rhs_ref.shape
    rows = cells_x + 2 * HALO
    tiles = cells_y // LANES
    me_x, me_y = lax.axis_index("gx"), lax.axis_index("gy")

    def device(side):
        return (
            lax.rem(me_x + side[0] + count_x, count_x),
            lax.rem(me_y + side[1] + count_y, count_y),
        )

    half = count_y // 2
    last = count_x - 1

    def over_y_seam(y, dy):
        return {-1: lax.rem(y, half) == 0, 0: y < 0, 1: lax.rem(y, half) == half - 1}[dy]

    def over(side):
        over_x = {-1: me_x == 0, 0: me_x < 0, 1: me_x == last}[side[0]]
        over_y = over_y_seam(me_y, side[1])
        return over_x & jnp.logical_not(over_y), over_y & jnp.logical_not(over_x)

    def at_y_seam(y):
        return (lax.rem(y, half) == 0) | (lax.rem(y, half) == half - 1)

    def by_token(x, y, over_x, over_y):
        return (over_x & (x == 0) & ((y < half) | at_y_seam(y))) | (over_y & (x == last) & (y < half))

    def signal(semaphore, target):
        pl.semaphore_signal(
            semaphore, inc=1, device_id=target, device_id_type=pl.DeviceIdType.MESH
        )

    def number(conditions):
        total = jnp.int32(0)
        for condition in conditions:
            total = total + condition.astype(jnp.int32)
        return total

    inner_y = me_y + 1 - 2 * lax.rem(me_y, 2)
    barrier = pltpu.get_barrier_semaphore()
    for side in SIDES:
        target = device(side)
        pl.when(jnp.logical_not(by_token(*target, *over(side))))(
            functools.partial(signal, barrier, target)
        )

    def turned(value, slot):
        value = value.reshape(levels * cells_x, cells_y)
        for t in range(tiles):
            turn[slot, t] = value[:, t * LANES : (t + 1) * LANES]
        return [
            [turn[slot, t, pl.ds(x, levels, stride=cells_x), :] for t in range(tiles)]
            for x in range(cells_x)
        ]

    def spread(t):
        return slice(t * LANES, (t + 1) * LANES)

    for load in loads:
        load.wait()
    for n, i in enumerate(ORDER):
        if i >= 0:
            value = coeffs_ref[i].astype(jnp.float32) * WEIGHTS[i]
        elif n == SIGMA:
            value = sigma_ref[...]
        elif n == RHS_HIGH:
            value = rhs_ref[...].astype(jnp.bfloat16).astype(jnp.float32)
        else:
            value = rhs_ref[...] - rhs_ref[...].astype(jnp.bfloat16).astype(jnp.float32)
        for x, parts in enumerate(turned(value, n)):
            for t, part in enumerate(parts):
                sent[HALO + x, n, :, spread(t)] = part.astype(jnp.bfloat16)

    lane = lax.broadcasted_iota(jnp.int32, (levels, LANES), 1)

    def pack(x, carry):
        low = jnp.zeros((levels, LANES), jnp.float32)
        high = jnp.zeros((levels, LANES), jnp.float32)
        for n in range(SENT):
            here = (lane >= HALO * n) & (lane < HALO * (n + 1))
            first = sent[HALO + x, n, :, :LANES].astype(jnp.float32)
            last = sent[HALO + x, n, :, cells_y - LANES : cells_y].astype(jnp.float32)
            low = jnp.where(here, roll(first, HALO * n, 1), low)
            high = jnp.where(here, roll(last, HALO * n + HALO, 1), high)
        packed_low[x] = low.astype(jnp.bfloat16)
        packed_high[x] = high.astype(jnp.bfloat16)
        return carry

    lax.fori_loop(0, cells_x, pack, 0)

    waiting = [by_token(me_x, me_y, *over(side)) for side in SIDES]
    pl.semaphore_wait(barrier, len(SIDES) - number(waiting))
    for side in SIDES:
        tell = over(side)[0] & (me_x == last) & (me_y < half)
        pl.when(tell)(functools.partial(signal, token.at[0], device(side)))
    at_corner = (me_x == 0) & (me_y >= half) & at_y_seam(me_y)
    pl.when((me_x == 0) & (me_y >= half) & at_y_seam(inner_y))(
        lambda: signal(token.at[0], (me_x, inner_y))
    )
    pl.when((me_x == last - 1) & (me_y < half) & at_y_seam(me_y))(
        lambda: signal(token.at[1], (last, me_y))
    )

    def remote(source, target, send, recv, side):
        return pltpu.make_async_remote_copy(
            src_ref=source,
            dst_ref=target,
            send_sem=send,
            recv_sem=recv,
            device_id=device(side),
            device_id_type=pl.DeviceIdType.MESH,
        )

    small, rowwise = [], {}
    for n, side in enumerate(SIDES):
        dx, dy = side
        if dy == 0:
            continue
        first, there = {-1: (0, HALO + cells_x), 0: (0, HALO), 1: (cells_x - HALO, 0)}[dx]
        count = cells_x if dx == 0 else HALO
        own, other = (packed_low, from_high) if dy == -1 else (packed_high, from_low)
        small.append(
            (
                side,
                remote(
                    own.at[pl.ds(first, count)],
                    other.at[pl.ds(there, count)],
                    send_sem.at[n],
                    recv_sem.at[n],
                    side,
                ),
            )
        )
    for away in range(1, HALO + 1):
        for k, dx in enumerate((-1, 1)):
            if dx == -1:
                source, target = HALO + away - 1, HALO + cells_x + away - 1
            else:
                source, target = HALO + cells_x - away, HALO - away
            fields = pl.ds(0, SENT)
            if away == HALO:
                fields = pl.ds(0 if dx == 1 else RHS_HIGH, OUTER)
            rowwise[dx, away] = remote(
                sent.at[source, fields, :, pl.ds(0, cells_y)],
                sent.at[target, fields, :, pl.ds(0, cells_y)],
                row_send_sem.at[k, away - 1],
                row_recv_sem.at[k, away - 1],
                (dx, 0),
            )
    copies = small + [((dx, 0), copy) for (dx, _), copy in rowwise.items()]

    later = {side: by for side, by in zip(SIDES, waiting)}
    for side, copy in copies:
        pl.when(jnp.logical_not(later[side]))(copy.start)
    for k in (0, 1):
        mine = {side: over(side)[k] & later[side] for side in SIDES}
        tokens = number(mine.values())
        tokens = jnp.where(at_corner, 1, tokens) if k == 0 else jnp.minimum(tokens, 1)

        @pl.when(tokens > 0)
        def _(mine=mine, tokens=tokens, k=k):
            pl.semaphore_wait(token.at[k], tokens)
            for side, copy in copies:
                pl.when(mine[side])(copy.start)

    theta = (LMAX + LMIN) / 2.0
    delta = (LMAX - LMIN) / 2.0
    s_one = theta / delta

    EVERY = range(SENT)
    main, strip = slice(0, cells_y), slice(cells_y, cells_y + LANES)

    def begin(row, at, right):
        residue[row, :, at] = right
        direction[0, row, :, at] = right * (1.0 / theta)
        pressure[row, :, at] = right * (1.0 / theta)

    def take(row, at, field, wanted):
        total = field(SIGMA) if len(wanted) == SENT else None
        for n in wanted:
            i = ORDER[n]
            if i >= 0:
                value = field(n)
                if total is not None:
                    total = total + value
                if OFFSETS[i][0] != 0:
                    value = jnp.where(leaves(OFFSETS[i][0], value.shape), 0.0, value)
                terms[row, n, :, at] = value
        if total is not None:
            diag[row, :, at] = total
        begin(row, at, field(RHS_HIGH) + field(RHS_LOW))

    def fields_of(row):
        if row == 0:
            return range(OUTER)
        return range(RHS_HIGH, RHS_HIGH + OUTER) if row == rows - 1 else EVERY

    EDGE, MIDDLE = 2 * HALO, LANES // 2

    def own_ends(row):
        for n in fields_of(row):
            low = sent[row, n, :, :LANES].astype(jnp.float32)
            high = sent[row, n, :, cells_y - LANES : cells_y].astype(jnp.float32)
            ends[row, n] = jnp.where(
                lane < MIDDLE, roll(high, EDGE, 1), roll(low, MIDDLE + HALO, 1)
            )

    def take_strip(row):
        above = from_high[row].astype(jnp.float32)
        below = from_low[row].astype(jnp.float32)
        is_above = (lane >= EDGE) & (lane < EDGE + HALO)
        is_below = (lane >= MIDDLE) & (lane < MIDDLE + HALO)

        def field(n):
            value = jnp.where(is_above, roll(above, EDGE - HALO * n, 1), ends[row, n])
            return jnp.where(is_below, roll(below, MIDDLE - HALO * n, 1), value)

        take(row, strip, field, fields_of(row))

    def take_main(row):
        take(row, main, lambda n: sent[row, n, :, :cells_y].astype(jnp.float32), fields_of(row))

    for x in range(cells_x):

        def exact(n):
            return jnp.concatenate(
                [turn[n, t, pl.ds(x, levels, stride=cells_x), :] for t in range(tiles)], axis=1
            )

        take(HALO + x, main, exact, EVERY)
        own_ends(HALO + x)

    factors = []
    rho = 1.0 / s_one
    for sweep in range(APPLIES):
        rho_new = 1.0 / (2.0 * s_one - rho)
        factors.append((rho_new * rho, 2.0 * rho_new / delta))
        rho = rho_new

    def apply(sweep, row, at):
        field = {k: direction[sweep - 1, row + k, :, at] for k in (-1, 0, 1)}

        def along(step_z, step_y):
            total = None
            for step_x in (-1, 0, 1):
                n = PLACE.get((step_z, step_x, step_y))
                if n is not None:
                    term = terms[row - step_x, n, :, at] * field[-step_x]
                    total = term if total is None else total + term
            return total

        def levels_moved(step_y):
            return roll(along(1, step_y), 1, 0) + roll(along(-1, step_y), -1, 0)

        total = along(0, 0) + levels_moved(0)
        total = total + roll(along(0, 1) + levels_moved(1), 1, 1)
        total = total + roll(along(0, -1) + levels_moved(-1), -1, 1)
        left = residue[row, :, at] - (diag[row, :, at] * field[0] - total)
        keep, add = factors[sweep - 1]
        value = keep * field[0] + add * left
        return row, at, left, value, pressure[row, :, at] + value

    def apply_rows(sweep, which, lanes):
        done = [apply(sweep, row, at) for row in which for at in lanes]
        for row, at, left, value, summed in done:
            residue[row, :, at] = left
            direction[sweep, row, :, at] = value
            pressure[row, :, at] = summed

    def wave(away, lanes):
        low, high = HALO - away, HALO + cells_x - 1 + away
        for sweep in range(1, APPLIES + 1):
            first, last_row = low + sweep, high - sweep
            if first < last_row:
                if away == 0:
                    for row in range(first, last_row, 2):
                        apply_rows(sweep, (row, row + 1), lanes)
                else:
                    apply_rows(sweep, (first, last_row), lanes)

    def rows_of(away):
        return ((1, HALO - away), (-1, HALO + cells_x - 1 + away))

    def receive_rows(away):
        for dx, row in rows_of(away):
            rowwise[dx, away].wait_recv()
            take_main(row)
            own_ends(row)

    far = at_y_seam(me_y)

    @pl.when(jnp.logical_not(far))
    def _():
        for _, copy in small:
            copy.wait_recv()
        for x in range(cells_x):
            take_strip(HALO + x)
        wave(0, (main, strip))
        for away in range(1, HALO + 1):
            receive_rows(away)
            for _, row in rows_of(away):
                take_strip(row)
            wave(away, (main, strip))

    @pl.when(far)
    def _():
        wave(0, (main,))
        for away in range(1, HALO + 1):
            receive_rows(away)
            wave(away, (main,))
        for _, copy in small:
            copy.wait_recv()
        for row in range(rows):
            take_strip(row)
        for sweep in range(1, APPLIES + 1):
            for row in range(sweep, rows - sweep, 2):
                apply_rows(sweep, (row, row + 1), (strip,))

    for n in range(cells_x + 2):
        row = HALO - 1 + n
        at_ends = pressure[row, :, strip]
        low, high = pressure[row, :, :LANES], pressure[row, :, cells_y - LANES : cells_y]
        low = jnp.where(lane < HALO, roll(at_ends, -MIDDLE - HALO, 1), low)
        high = jnp.where(lane >= LANES - HALO, roll(at_ends, -EDGE, 1), high)
        beyond = jnp.where(
            lane < MIDDLE, roll(at_ends, -EDGE, 1), roll(at_ends, LANES - MIDDLE - HALO, 1)
        )
        pressure_ref[n, :, :cells_y] = pressure[row, :, :cells_y]
        pressure_ref[n, :, :LANES] = low
        pressure_ref[n, :, cells_y - LANES : cells_y] = high
        pressure_ref[n, :, cells_y:] = beyond

    for _, copy in copies:
        copy.wait_send()


def leaves(step_z, shape):
    level = lax.broadcasted_iota(jnp.int32, shape, 0)
    return level == (shape[0] - 1 if step_z == 1 else 0)


def correct(pressure, vel_ref, metric_ref, pressure_ref, out_ref, turn):
    levels, cells_x, cells_y = pressure_ref.shape
    tiles = cells_y // LANES
    shape = pressure.shape[1:]
    for x in range(cells_x):
        here = pressure[x + 1]
        grad_x = (pressure[x + 2] - pressure[x]) * 0.5
        grad_y = (roll(here, -1, 1) - roll(here, 1, 1)) * 0.5
        upper = jnp.where(leaves(1, shape), 0.0, roll(here, -1, 0))
        lower = jnp.where(leaves(-1, shape), 0.0, roll(here, 1, 0))
        grad_z = (upper - lower) * 0.5
        for n, value in enumerate((grad_x, grad_y, grad_z, here)):
            for t in range(tiles):
                turn[n, t, pl.ds(x * levels, levels), :] = value[:, t * LANES : (t + 1) * LANES]
    for z in range(levels):
        for t in range(tiles):
            at = slice(t * LANES, (t + 1) * LANES)
            back = [turn[n, t, pl.ds(z, cells_x, stride=levels), :] for n in range(4)]
            pressure_ref[z, :, at] = back[3]
            for n in range(3):
                out_ref[n, z, :, at] = (
                    vel_ref[n, z, :, at].astype(jnp.float32)
                    - metric_ref[n, z, :, at].astype(jnp.float32) * back[n]
                )


def on_device(count_x, count_y, coeffs, sigma, rhs, vel_bar, metric):
    levels, cells_x, cells_y = rhs.shape
    rows, width = cells_x + 2 * HALO, cells_y + LANES
    vmem = pl.BlockSpec(memory_space=pltpu.VMEM)
    hbm = pl.BlockSpec(memory_space=pltpu.HBM)
    pressure = pl.pallas_call(
        functools.partial(kernel, count_x, count_y),
        out_shape=jax.ShapeDtypeStruct((cells_x + 2, levels, width), jnp.float32),
        in_specs=[hbm] * 3,
        out_specs=vmem,
        scratch_shapes=[
            pltpu.VMEM(coeffs.shape, jnp.bfloat16),
            pltpu.VMEM(sigma.shape, jnp.float32),
            pltpu.VMEM(rhs.shape, jnp.float32),
            pltpu.SemaphoreType.DMA((3,)),
            pltpu.VMEM((rows, SENT, levels, width), jnp.bfloat16),
            pltpu.VMEM((cells_x, levels, LANES), jnp.bfloat16),
            pltpu.VMEM((cells_x, levels, LANES), jnp.bfloat16),
            pltpu.VMEM((rows, levels, LANES), jnp.bfloat16),
            pltpu.VMEM((rows, levels, LANES), jnp.bfloat16),
            pltpu.VMEM((rows, SENT, levels, width), jnp.float32),
            pltpu.VMEM((rows, SENT, levels, LANES), jnp.float32),
            pltpu.VMEM((rows, levels, width), jnp.float32),
            pltpu.VMEM((SENT, cells_y // LANES, levels * cells_x, LANES), jnp.float32),
            pltpu.VMEM((SWEEPS, rows, levels, width), jnp.float32),
            pltpu.VMEM((rows, levels, width), jnp.float32),
            pltpu.VMEM((rows, levels, width), jnp.float32),
            pltpu.SemaphoreType.DMA((len(SIDES),)),
            pltpu.SemaphoreType.DMA((len(SIDES),)),
            pltpu.SemaphoreType.DMA((2, HALO)),
            pltpu.SemaphoreType.DMA((2, HALO)),
            pltpu.SemaphoreType.REGULAR((2,)),
        ],
        compiler_params=pltpu.CompilerParams(
            collective_id=0, has_side_effects=True, vmem_limit_bytes=66519040
        ),
    )(coeffs, sigma, rhs)
    return pl.pallas_call(
        correct,
        out_shape=(
            jax.ShapeDtypeStruct(rhs.shape, jnp.float32),
            jax.ShapeDtypeStruct(vel_bar.shape, jnp.float32),
        ),
        in_specs=[vmem] * 3,
        out_specs=(vmem, vmem),
        scratch_shapes=[pltpu.VMEM((4, cells_y // LANES, levels * cells_x, LANES), jnp.float32)],
        compiler_params=pltpu.CompilerParams(vmem_limit_bytes=8 << 20),
    )(pressure, vel_bar, metric)


def solution(mesh):
    return jax.shard_map(
        functools.partial(on_device, mesh.shape["gx"], mesh.shape["gy"]),
        mesh=mesh,
        in_specs=(
            P(None, None, "gx", "gy"),
            P(None, "gx", "gy"),
            P(None, "gx", "gy"),
            P(None, None, "gx", "gy"),
            P(None, None, "gx", "gy"),
        ),
        out_specs=(P(None, "gx", "gy"), P(None, None, "gx", "gy")),
        check_vma=False,
    )
```

```python
import functools

import jax
import jax.numpy as jnp
from jax import lax
from jax.experimental import pallas as pl
from jax.experimental.pallas import tpu as pltpu
from jax.sharding import PartitionSpec as P

SWEEPS = 6
APPLIES = SWEEPS - 1
HALO = APPLIES + 1
LMIN, LMAX = 0.5, 31.0
LANES = 128
DIRECT = HALO // 2

OFFSETS = (
    (1, 0, 0),
    (-1, 0, 0),
    (0, 1, 0),
    (0, -1, 0),
    (0, 0, 1),
    (0, 0, -1),
    (0, 1, 1),
    (0, 1, -1),
    (0, -1, 1),
    (0, -1, -1),
    (1, 1, 0),
    (1, -1, 0),
    (-1, 1, 0),
    (-1, -1, 0),
    (1, 0, 1),
    (1, 0, -1),
    (-1, 0, 1),
    (-1, 0, -1),
)
WEIGHTS = (1.0,) * 6 + (0.25,) * 12
TERMS = len(OFFSETS)
ORDER = (
    [i for i in range(TERMS) if OFFSETS[i][1] == 1]
    + [-1, -2]
    + [i for i in range(TERMS) if OFFSETS[i][1] == -1]
    + [i for i in range(TERMS) if OFFSETS[i][1] == 0]
    + [-3]
)
SENT = len(ORDER)
RHS_HIGH, RHS_LOW, SIGMA = ORDER.index(-1), ORDER.index(-2), ORDER.index(-3)
PLACE = {OFFSETS[i]: n for n, i in enumerate(ORDER) if i >= 0}
OUTER = RHS_LOW + 1
SIDES = ((0, -1), (0, 1), (-1, -1), (-1, 1), (1, -1), (1, 1), (-1, 0), (1, 0))


def roll(value, shift, axis):
    size = value.shape[axis]
    return pltpu.roll(value, shift % size, axis)


def kernel(
    count_x,
    count_y,
    coeffs_hbm,
    sigma_hbm,
    rhs_hbm,
    pressure_ref,
    coeffs_ref,
    sigma_ref,
    rhs_ref,
    load_sem,
    sent,
    packed_low,
    packed_high,
    from_high,
    from_low,
    terms,
    ends,
    diag,
    turn,
    direction,
    residue,
    pressure,
    send_sem,
    recv_sem,
    row_send_sem,
    row_recv_sem,
    forward_sem,
    token,
):
    loads = [
        pltpu.make_async_copy(source, target, load_sem.at[n])
        for n, (source, target) in enumerate(
            ((coeffs_hbm, coeffs_ref), (sigma_hbm, sigma_ref), (rhs_hbm, rhs_ref))
        )
    ]
    for load in loads:
        load.start()
    levels, cells_x, cells_y = rhs_ref.shape
    rows = cells_x + 2 * HALO
    tiles = cells_y // LANES
    me_x, me_y = lax.axis_index("gx"), lax.axis_index("gy")

    def device(side):
        return (
            lax.rem(me_x + side[0] + count_x, count_x),
            lax.rem(me_y + side[1] + count_y, count_y),
        )

    half = count_y // 2
    last = count_x - 1

    def over_y_seam(y, dy):
        return {-1: lax.rem(y, half) == 0, 0: y < 0, 1: lax.rem(y, half) == half - 1}[dy]

    def over(side):
        over_x = {-1: me_x == 0, 0: me_x < 0, 1: me_x == last}[side[0]]
        over_y = over_y_seam(me_y, side[1])
        return over_x & jnp.logical_not(over_y), over_y & jnp.logical_not(over_x)

    def at_y_seam(y):
        return (lax.rem(y, half) == 0) | (lax.rem(y, half) == half - 1)

    def by_token(x, y, over_x, over_y):
        return (over_x & (x == 0) & ((y < half) | at_y_seam(y))) | (over_y & (x == last) & (y < half))

    def signal(semaphore, target):
        pl.semaphore_signal(
            semaphore, inc=1, device_id=target, device_id_type=pl.DeviceIdType.MESH
        )

    def number(conditions):
        total = jnp.int32(0)
        for condition in conditions:
            total = total + condition.astype(jnp.int32)
        return total

    inner_y = me_y + 1 - 2 * lax.rem(me_y, 2)
    barrier = pltpu.get_barrier_semaphore()
    for side in SIDES:
        target = device(side)
        pl.when(jnp.logical_not(by_token(*target, *over(side))))(
            functools.partial(signal, barrier, target)
        )

    for x, to in ((0, last - 1), (1, last)):
        pl.when(me_x == x)(functools.partial(signal, barrier, (to, me_y)))

    def turned(value, slot):
        value = value.reshape(levels * cells_x, cells_y)
        for t in range(tiles):
            turn[slot, t] = value[:, t * LANES : (t + 1) * LANES]
        return [
            [turn[slot, t, pl.ds(x, levels, stride=cells_x), :] for t in range(tiles)]
            for x in range(cells_x)
        ]

    def spread(t):
        return slice(t * LANES, (t + 1) * LANES)

    for load in loads:
        load.wait()
    for n, i in enumerate(ORDER):
        if i >= 0:
            value = coeffs_ref[i].astype(jnp.float32) * WEIGHTS[i]
        elif n == SIGMA:
            value = sigma_ref[...]
        elif n == RHS_HIGH:
            value = rhs_ref[...].astype(jnp.bfloat16).astype(jnp.float32)
        else:
            value = rhs_ref[...] - rhs_ref[...].astype(jnp.bfloat16).astype(jnp.float32)
        for x, parts in enumerate(turned(value, n)):
            for t, part in enumerate(parts):
                sent[HALO + x, n, :, spread(t)] = part.astype(jnp.bfloat16)

    lane = lax.broadcasted_iota(jnp.int32, (levels, LANES), 1)

    def pack(x, carry):
        low = jnp.zeros((levels, LANES), jnp.float32)
        high = jnp.zeros((levels, LANES), jnp.float32)
        for n in range(SENT):
            here = (lane >= HALO * n) & (lane < HALO * (n + 1))
            first = sent[HALO + x, n, :, :LANES].astype(jnp.float32)
            last = sent[HALO + x, n, :, cells_y - LANES : cells_y].astype(jnp.float32)
            low = jnp.where(here, roll(first, HALO * n, 1), low)
            high = jnp.where(here, roll(last, HALO * n + HALO, 1), high)
        packed_low[x] = low.astype(jnp.bfloat16)
        packed_high[x] = high.astype(jnp.bfloat16)
        return carry

    lax.fori_loop(0, cells_x, pack, 0)

    waiting = [by_token(me_x, me_y, *over(side)) for side in SIDES]
    forwarded_to = number([me_x == last - 1, me_x == last])
    pl.semaphore_wait(barrier, len(SIDES) + forwarded_to - number(waiting))
    pl.when(me_x == last)(lambda: signal(token.at[2], (1, me_y)))
    for side in SIDES:
        tell = over(side)[0] & (me_x == last) & (me_y < half)
        pl.when(tell)(functools.partial(signal, token.at[0], device(side)))
    at_corner = (me_x == 0) & (me_y >= half) & at_y_seam(me_y)
    pl.when((me_x == 0) & (me_y >= half) & at_y_seam(inner_y))(
        lambda: signal(token.at[0], (me_x, inner_y))
    )
    pl.when((me_x == last - 1) & (me_y < half) & at_y_seam(me_y))(
        lambda: signal(token.at[1], (last, me_y))
    )

    def remote(source, target, send, recv, side):
        return pltpu.make_async_remote_copy(
            src_ref=source,
            dst_ref=target,
            send_sem=send,
            recv_sem=recv,
            device_id=device(side),
            device_id_type=pl.DeviceIdType.MESH,
        )

    small, rowwise = [], {}
    for n, side in enumerate(SIDES):
        dx, dy = side
        if dy == 0:
            continue
        first, there = {-1: (0, HALO + cells_x), 0: (0, HALO), 1: (cells_x - HALO, 0)}[dx]
        count = cells_x if dx == 0 else HALO
        own, other = (packed_low, from_high) if dy == -1 else (packed_high, from_low)
        small.append(
            (
                side,
                remote(
                    own.at[pl.ds(first, count)],
                    other.at[pl.ds(there, count)],
                    send_sem.at[n],
                    recv_sem.at[n],
                    side,
                ),
            )
        )
    for away in range(1, HALO + 1):
        for k, dx in enumerate((-1, 1)):
            if dx == -1:
                source, target = HALO + away - 1, HALO + cells_x + away - 1
            else:
                source, target = HALO + cells_x - away, HALO - away
            fields = pl.ds(0, SENT)
            if away == HALO:
                fields = pl.ds(0 if dx == 1 else RHS_HIGH, OUTER)
            rowwise[dx, away] = remote(
                sent.at[source, fields, :, pl.ds(0, cells_y)],
                sent.at[target, fields, :, pl.ds(0, cells_y)],
                row_send_sem.at[k, away - 1],
                row_recv_sem.at[k, away - 1],
                (dx, 0),
            )
    def fields_at(dx, away):
        return pl.ds(0, SENT) if away < HALO else pl.ds(0 if dx == 1 else RHS_HIGH, OUTER)

    forwards = {1: [], -1: []}
    for away in range(DIRECT + 1, HALO + 1):
        for k, dx in enumerate((-1, 1)):
            width = pl.ds(0, cells_y)
            if dx == 1:
                source, target, to = HALO + 2 * cells_x - away, HALO - away, 0
            else:
                source, target, to = HALO - cells_x + away - 1, HALO + cells_x + away - 1, last
            copy = pltpu.make_async_remote_copy(
                src_ref=sent.at[source, fields_at(dx, away), :, width],
                dst_ref=sent.at[target, fields_at(dx, away), :, width],
                send_sem=forward_sem.at[k, away - DIRECT - 1],
                recv_sem=row_recv_sem.at[k, away - 1],
                device_id=(to, me_y),
                device_id_type=pl.DeviceIdType.MESH,
            )
            forwards[dx].append((cells_x + 1 - away, copy))
    forwarder = {1: me_x == last - 1, -1: me_x == 1}

    copies = [(side, copy, True) for side, copy in small]
    first_rows = [cells_x + 1 - away for away in range(DIRECT + 1, HALO + 1)]
    at_end = {1: me_x == last, -1: me_x == 0}
    for dx in (-1, 1):
        for away in first_rows:
            copies.append(((dx, 0), rowwise[dx, away], at_end[-dx]))
    for (dx, away), copy in rowwise.items():
        sends = True
        if away in first_rows:
            sends = jnp.logical_not(at_end[-dx])
        if away > DIRECT:
            sends = sends & jnp.logical_not(at_end[dx])
        copies.append(((dx, 0), copy, sends))

    later = {side: by for side, by in zip(SIDES, waiting)}
    for side, copy, sends in copies:
        pl.when(jnp.logical_not(later[side]) & sends)(copy.start)
    for k in (0, 1):
        mine = {side: over(side)[k] & later[side] for side in SIDES}
        tokens = number(mine.values())
        tokens = jnp.where(at_corner, 1, tokens) if k == 0 else jnp.minimum(tokens, 1)

        @pl.when(tokens > 0)
        def _(mine=mine, tokens=tokens, k=k):
            pl.semaphore_wait(token.at[k], tokens)
            for side, copy, sends in copies:
                pl.when(mine[side] & sends)(copy.start)

    def forward(dx):
        for away, copy in forwards[dx]:
            rowwise[-dx, away].wait_recv()
            copy.start()

    pl.when(forwarder[1])(lambda: forward(1))

    def forward_back():
        pl.semaphore_wait(token.at[2], 1)
        forward(-1)

    theta = (LMAX + LMIN) / 2.0
    delta = (LMAX - LMIN) / 2.0
    s_one = theta / delta

    EVERY = range(SENT)
    main, strip = slice(0, cells_y), slice(cells_y, cells_y + LANES)

    def begin(row, at, right):
        residue[row, :, at] = right
        direction[0, row, :, at] = right * (1.0 / theta)
        pressure[row, :, at] = right * (1.0 / theta)

    def take(row, at, field, wanted):
        total = field(SIGMA) if len(wanted) == SENT else None
        for n in wanted:
            i = ORDER[n]
            if i >= 0:
                value = field(n)
                if total is not None:
                    total = total + value
                if OFFSETS[i][0] != 0:
                    value = jnp.where(leaves(OFFSETS[i][0], value.shape), 0.0, value)
                terms[row, n, :, at] = value
        if total is not None:
            diag[row, :, at] = total
        begin(row, at, field(RHS_HIGH) + field(RHS_LOW))

    def fields_of(row):
        if row == 0:
            return range(OUTER)
        return range(RHS_HIGH, RHS_HIGH + OUTER) if row == rows - 1 else EVERY

    EDGE, MIDDLE = 2 * HALO, LANES // 2

    def own_ends(row, field):
        for n in fields_of(row):
            low, high = field(n, 0), field(n, tiles - 1)
            ends[row, n] = jnp.where(
                lane < MIDDLE, roll(high, EDGE, 1), roll(low, MIDDLE + HALO, 1)
            )

    def take_strip(row):
        above = from_high[row].astype(jnp.float32)
        below = from_low[row].astype(jnp.float32)
        is_above = (lane >= EDGE) & (lane < EDGE + HALO)
        is_below = (lane >= MIDDLE) & (lane < MIDDLE + HALO)

        def field(n):
            value = jnp.where(is_above, roll(above, EDGE - HALO * n, 1), ends[row, n])
            return jnp.where(is_below, roll(below, MIDDLE - HALO * n, 1), value)

        take(row, strip, field, fields_of(row))

    def take_main(row, field):
        take(
            row,
            main,
            lambda n: jnp.concatenate([field(n, t) for t in range(tiles)], axis=1),
            fields_of(row),
        )
        own_ends(row, field)

    for x in range(cells_x):
        take_main(HALO + x, lambda n, t: turn[n, t, pl.ds(x, levels, stride=cells_x), :])

    factors = []
    rho = 1.0 / s_one
    for sweep in range(APPLIES):
        rho_new = 1.0 / (2.0 * s_one - rho)
        factors.append((rho_new * rho, 2.0 * rho_new / delta))
        rho = rho_new

    def apply(sweep, row, at):
        field = {k: direction[sweep - 1, row + k, :, at] for k in (-1, 0, 1)}

        def along(step_z, step_y):
            total = None
            for step_x in (-1, 0, 1):
                n = PLACE.get((step_z, step_x, step_y))
                if n is not None:
                    term = terms[row - step_x, n, :, at] * field[-step_x]
                    total = term if total is None else total + term
            return total

        def levels_moved(step_y):
            return roll(along(1, step_y), 1, 0) + roll(along(-1, step_y), -1, 0)

        total = along(0, 0) + levels_moved(0)
        total = total + roll(along(0, 1) + levels_moved(1), 1, 1)
        total = total + roll(along(0, -1) + levels_moved(-1), -1, 1)
        left = residue[row, :, at] - (diag[row, :, at] * field[0] - total)
        keep, add = factors[sweep - 1]
        value = keep * field[0] + add * left
        return row, at, left, value, pressure[row, :, at] + value

    def apply_rows(sweep, which, lanes):
        done = [apply(sweep, row, at) for row in which for at in lanes]
        for row, at, left, value, summed in done:
            residue[row, :, at] = left
            direction[sweep, row, :, at] = value
            pressure[row, :, at] = summed

    def wave(away, lanes):
        low, high = HALO - away, HALO + cells_x - 1 + away
        for sweep in range(1, APPLIES + 1):
            first, last_row = low + sweep, high - sweep
            if first < last_row:
                if away == 0:
                    for row in range(first, last_row, 2):
                        apply_rows(sweep, (row, row + 1), lanes)
                else:
                    apply_rows(sweep, (first, last_row), lanes)

    def rows_of(away):
        return ((1, HALO - away), (-1, HALO + cells_x - 1 + away))

    def receive_rows(away):
        for dx, row in rows_of(away):
            if away in first_rows:
                pl.when(jnp.logical_not(forwarder[-dx]))(rowwise[dx, away].wait_recv)
            else:
                rowwise[dx, away].wait_recv()
            take_main(row, lambda n, t: sent[row, n, :, spread(t)].astype(jnp.float32))

    pl.when(forwarder[-1])(forward_back)

    far = at_y_seam(me_y)

    @pl.when(jnp.logical_not(far))
    def _():
        for _, copy in small:
            copy.wait_recv()
        for x in range(cells_x):
            take_strip(HALO + x)
        wave(0, (main, strip))
        for away in range(1, HALO + 1):
            receive_rows(away)
            for _, row in rows_of(away):
                take_strip(row)
            wave(away, (main, strip))

    @pl.when(far)
    def _():
        wave(0, (main,))
        for away in range(1, HALO + 1):
            receive_rows(away)
            wave(away, (main,))
        for _, copy in small:
            copy.wait_recv()
        for row in range(rows):
            take_strip(row)
        for sweep in range(1, APPLIES + 1):
            for row in range(sweep, rows - sweep, 2):
                apply_rows(sweep, (row, row + 1), (strip,))

    for n in range(cells_x + 2):
        row = HALO - 1 + n
        at_ends = pressure[row, :, strip]
        low, high = pressure[row, :, :LANES], pressure[row, :, cells_y - LANES : cells_y]
        low = jnp.where(lane < HALO, roll(at_ends, -MIDDLE - HALO, 1), low)
        high = jnp.where(lane >= LANES - HALO, roll(at_ends, -EDGE, 1), high)
        beyond = jnp.where(
            lane < MIDDLE, roll(at_ends, -EDGE, 1), roll(at_ends, LANES - MIDDLE - HALO, 1)
        )
        pressure_ref[n, :, :cells_y] = pressure[row, :, :cells_y]
        pressure_ref[n, :, :LANES] = low
        pressure_ref[n, :, cells_y - LANES : cells_y] = high
        pressure_ref[n, :, cells_y:] = beyond

    for _, copy, sends in copies:
        (copy.wait_send() if sends is True else pl.when(sends)(copy.wait_send))
    for dx in (1, -1):
        for _, copy in forwards[dx]:
            pl.when(forwarder[dx])(copy.wait_send)


def leaves(step_z, shape):
    level = lax.broadcasted_iota(jnp.int32, shape, 0)
    return level == (shape[0] - 1 if step_z == 1 else 0)


def correct(pressure, vel_ref, metric_ref, pressure_ref, out_ref, turn):
    levels, cells_x, cells_y = pressure_ref.shape
    tiles = cells_y // LANES
    shape = pressure.shape[1:]
    for x in range(cells_x):
        here = pressure[x + 1]
        grad_x = (pressure[x + 2] - pressure[x]) * 0.5
        grad_y = (roll(here, -1, 1) - roll(here, 1, 1)) * 0.5
        upper = jnp.where(leaves(1, shape), 0.0, roll(here, -1, 0))
        lower = jnp.where(leaves(-1, shape), 0.0, roll(here, 1, 0))
        grad_z = (upper - lower) * 0.5
        for n, value in enumerate((grad_x, grad_y, grad_z, here)):
            for t in range(tiles):
                turn[n, t, pl.ds(x * levels, levels), :] = value[:, t * LANES : (t + 1) * LANES]
    for z in range(levels):
        for t in range(tiles):
            at = slice(t * LANES, (t + 1) * LANES)
            back = [turn[n, t, pl.ds(z, cells_x, stride=levels), :] for n in range(4)]
            pressure_ref[z, :, at] = back[3]
            for n in range(3):
                out_ref[n, z, :, at] = (
                    vel_ref[n, z, :, at].astype(jnp.float32)
                    - metric_ref[n, z, :, at].astype(jnp.float32) * back[n]
                )


def on_device(count_x, count_y, coeffs, sigma, rhs, vel_bar, metric):
    levels, cells_x, cells_y = rhs.shape
    rows, width = cells_x + 2 * HALO, cells_y + LANES
    vmem = pl.BlockSpec(memory_space=pltpu.VMEM)
    hbm = pl.BlockSpec(memory_space=pltpu.HBM)
    pressure = pl.pallas_call(
        functools.partial(kernel, count_x, count_y),
        out_shape=jax.ShapeDtypeStruct((cells_x + 2, levels, width), jnp.float32),
        in_specs=[hbm] * 3,
        out_specs=vmem,
        scratch_shapes=[
            pltpu.VMEM(coeffs.shape, jnp.bfloat16),
            pltpu.VMEM(sigma.shape, jnp.float32),
            pltpu.VMEM(rhs.shape, jnp.float32),
            pltpu.SemaphoreType.DMA((3,)),
            pltpu.VMEM((rows, SENT, levels, width), jnp.bfloat16),
            pltpu.VMEM((cells_x, levels, LANES), jnp.bfloat16),
            pltpu.VMEM((cells_x, levels, LANES), jnp.bfloat16),
            pltpu.VMEM((rows, levels, LANES), jnp.bfloat16),
            pltpu.VMEM((rows, levels, LANES), jnp.bfloat16),
            pltpu.VMEM((rows, SENT, levels, width), jnp.float32),
            pltpu.VMEM((rows, SENT, levels, LANES), jnp.float32),
            pltpu.VMEM((rows, levels, width), jnp.float32),
            pltpu.VMEM((SENT, cells_y // LANES, levels * cells_x, LANES), jnp.float32),
            pltpu.VMEM((SWEEPS, rows, levels, width), jnp.float32),
            pltpu.VMEM((rows, levels, width), jnp.float32),
            pltpu.VMEM((rows, levels, width), jnp.float32),
            pltpu.SemaphoreType.DMA((len(SIDES),)),
            pltpu.SemaphoreType.DMA((len(SIDES),)),
            pltpu.SemaphoreType.DMA((2, HALO)),
            pltpu.SemaphoreType.DMA((2, HALO)),
            pltpu.SemaphoreType.DMA((2, HALO - DIRECT)),
            pltpu.SemaphoreType.REGULAR((3,)),
        ],
        compiler_params=pltpu.CompilerParams(
            collective_id=0, has_side_effects=True, vmem_limit_bytes=32 << 20
        ),
    )(*(pltpu.with_memory_space_constraint(v, pltpu.HBM) for v in (coeffs, sigma, rhs)))
    return pl.pallas_call(
        correct,
        out_shape=(
            jax.ShapeDtypeStruct(rhs.shape, jnp.float32),
            jax.ShapeDtypeStruct(vel_bar.shape, jnp.float32),
        ),
        in_specs=[vmem] * 3,
        out_specs=(vmem, vmem),
        scratch_shapes=[pltpu.VMEM((4, cells_y // LANES, levels * cells_x, LANES), jnp.float32)],
        compiler_params=pltpu.CompilerParams(vmem_limit_bytes=8 << 20),
    )(pressure, vel_bar, metric)


def solution(mesh):
    return jax.shard_map(
        functools.partial(on_device, mesh.shape["gx"], mesh.shape["gy"]),
        mesh=mesh,
        in_specs=(
            P(None, None, "gx", "gy"),
            P(None, "gx", "gy"),
            P(None, "gx", "gy"),
            P(None, None, "gx", "gy"),
            P(None, None, "gx", "gy"),
        ),
        out_specs=(P(None, "gx", "gy"), P(None, None, "gx", "gy")),
        check_vma=False,
    )
```

```python
import functools

import jax
import jax.numpy as jnp
from jax import lax
from jax.experimental import pallas as pl
from jax.experimental.pallas import tpu as pltpu
from jax.sharding import PartitionSpec as P

SWEEPS = 6
APPLIES = SWEEPS - 1
HALO = APPLIES + 1
LMIN, LMAX = 0.5, 31.0
LANES = 128
DIRECT = HALO // 2

OFFSETS = (
    (1, 0, 0),
    (-1, 0, 0),
    (0, 1, 0),
    (0, -1, 0),
    (0, 0, 1),
    (0, 0, -1),
    (0, 1, 1),
    (0, 1, -1),
    (0, -1, 1),
    (0, -1, -1),
    (1, 1, 0),
    (1, -1, 0),
    (-1, 1, 0),
    (-1, -1, 0),
    (1, 0, 1),
    (1, 0, -1),
    (-1, 0, 1),
    (-1, 0, -1),
)
WEIGHTS = (1.0,) * 6 + (0.25,) * 12
TERMS = len(OFFSETS)
ORDER = (
    [i for i in range(TERMS) if OFFSETS[i][1] == 1]
    + [-1, -2]
    + [i for i in range(TERMS) if OFFSETS[i][1] == -1]
    + [i for i in range(TERMS) if OFFSETS[i][1] == 0]
    + [-3]
)
SENT = len(ORDER)
RHS_HIGH, RHS_LOW, SIGMA = ORDER.index(-1), ORDER.index(-2), ORDER.index(-3)
PLACE = {OFFSETS[i]: n for n, i in enumerate(ORDER) if i >= 0}
OUTER = RHS_LOW + 1
SIDES = ((0, -1), (0, 1), (-1, -1), (-1, 1), (1, -1), (1, 1), (-1, 0), (1, 0))


def roll(value, shift, axis):
    size = value.shape[axis]
    return pltpu.roll(value, shift % size, axis)


def kernel(
    count_x,
    count_y,
    coeffs_hbm,
    sigma_hbm,
    rhs_hbm,
    pressure_ref,
    coeffs_ref,
    sigma_ref,
    rhs_ref,
    load_sem,
    sent,
    packed_low,
    packed_high,
    from_high,
    from_low,
    terms,
    ends,
    diag,
    turn,
    direction,
    residue,
    pressure,
    send_sem,
    recv_sem,
    row_send_sem,
    row_recv_sem,
    forward_sem,
    token,
):
    loads = [
        pltpu.make_async_copy(source, target, load_sem.at[n])
        for n, (source, target) in enumerate(
            ((coeffs_hbm, coeffs_ref), (sigma_hbm, sigma_ref), (rhs_hbm, rhs_ref))
        )
    ]
    for load in loads:
        load.start()
    levels, cells_x, cells_y = rhs_ref.shape
    rows = cells_x + 2 * HALO
    tiles = cells_y // LANES
    me_x, me_y = lax.axis_index("gx"), lax.axis_index("gy")

    def device(side):
        return (
            lax.rem(me_x + side[0] + count_x, count_x),
            lax.rem(me_y + side[1] + count_y, count_y),
        )

    half = count_y // 2
    last = count_x - 1

    def over_y_seam(y, dy):
        return {-1: lax.rem(y, half) == 0, 0: y < 0, 1: lax.rem(y, half) == half - 1}[dy]

    def over(side):
        over_x = {-1: me_x == 0, 0: me_x < 0, 1: me_x == last}[side[0]]
        over_y = over_y_seam(me_y, side[1])
        return over_x & jnp.logical_not(over_y), over_y & jnp.logical_not(over_x)

    def at_y_seam(y):
        return (lax.rem(y, half) == 0) | (lax.rem(y, half) == half - 1)

    def by_token(x, y, over_x, over_y):
        return (over_x & (x == 0) & ((y < half) | at_y_seam(y))) | (over_y & (x == last) & (y < half))

    def signal(semaphore, target):
        pl.semaphore_signal(
            semaphore, inc=1, device_id=target, device_id_type=pl.DeviceIdType.MESH
        )

    def number(conditions):
        total = jnp.int32(0)
        for condition in conditions:
            total = total + condition.astype(jnp.int32)
        return total

    inner_y = me_y + 1 - 2 * lax.rem(me_y, 2)
    barrier = pltpu.get_barrier_semaphore()
    for side in SIDES:
        target = device(side)
        pl.when(jnp.logical_not(by_token(*target, *over(side))))(
            functools.partial(signal, barrier, target)
        )

    for x, to in ((0, last - 1), (1, last)):
        pl.when(me_x == x)(functools.partial(signal, barrier, (to, me_y)))

    def turned(value, slot):
        value = value.reshape(levels * cells_x, cells_y)
        for t in range(tiles):
            turn[slot, t] = value[:, t * LANES : (t + 1) * LANES]
        return [
            [turn[slot, t, pl.ds(x, levels, stride=cells_x), :] for t in range(tiles)]
            for x in range(cells_x)
        ]

    def spread(t):
        return slice(t * LANES, (t + 1) * LANES)

    for load in loads:
        load.wait()
    for n, i in enumerate(ORDER):
        if i >= 0:
            value = coeffs_ref[i].astype(jnp.float32) * WEIGHTS[i]
        elif n == SIGMA:
            value = sigma_ref[...]
        elif n == RHS_HIGH:
            value = rhs_ref[...].astype(jnp.bfloat16).astype(jnp.float32)
        else:
            value = rhs_ref[...] - rhs_ref[...].astype(jnp.bfloat16).astype(jnp.float32)
        for x, parts in enumerate(turned(value, n)):
            for t, part in enumerate(parts):
                sent[HALO + x, n, :, spread(t)] = part.astype(jnp.bfloat16)

    lane = lax.broadcasted_iota(jnp.int32, (levels, LANES), 1)

    def pack(x, carry):
        low = jnp.zeros((levels, LANES), jnp.float32)
        high = jnp.zeros((levels, LANES), jnp.float32)
        for n in range(SENT):
            here = (lane >= HALO * n) & (lane < HALO * (n + 1))
            first = sent[HALO + x, n, :, :LANES].astype(jnp.float32)
            last = sent[HALO + x, n, :, cells_y - LANES : cells_y].astype(jnp.float32)
            low = jnp.where(here, roll(first, HALO * n, 1), low)
            high = jnp.where(here, roll(last, HALO * n + HALO, 1), high)
        packed_low[x] = low.astype(jnp.bfloat16)
        packed_high[x] = high.astype(jnp.bfloat16)
        return carry

    lax.fori_loop(0, cells_x, pack, 0, unroll=True)

    waiting = [by_token(me_x, me_y, *over(side)) for side in SIDES]
    forwarded_to = number([me_x == last - 1, me_x == last])
    pl.semaphore_wait(barrier, len(SIDES) + forwarded_to - number(waiting))
    pl.when(me_x == last)(lambda: signal(token.at[2], (1, me_y)))
    for side in SIDES:
        tell = over(side)[0] & (me_x == last) & (me_y < half)
        pl.when(tell)(functools.partial(signal, token.at[0], device(side)))
    at_corner = (me_x == 0) & (me_y >= half) & at_y_seam(me_y)
    pl.when((me_x == 0) & (me_y >= half) & at_y_seam(inner_y))(
        lambda: signal(token.at[0], (me_x, inner_y))
    )
    pl.when((me_x == last - 1) & (me_y < half) & at_y_seam(me_y))(
        lambda: signal(token.at[1], (last, me_y))
    )

    def remote(source, target, send, recv, side):
        return pltpu.make_async_remote_copy(
            src_ref=source,
            dst_ref=target,
            send_sem=send,
            recv_sem=recv,
            device_id=device(side),
            device_id_type=pl.DeviceIdType.MESH,
        )

    small, rowwise = [], {}
    for n, side in enumerate(SIDES):
        dx, dy = side
        if dy == 0:
            continue
        first, there = {-1: (0, HALO + cells_x), 0: (0, HALO), 1: (cells_x - HALO, 0)}[dx]
        count = cells_x if dx == 0 else HALO
        own, other = (packed_low, from_high) if dy == -1 else (packed_high, from_low)
        small.append(
            (
                side,
                remote(
                    own.at[pl.ds(first, count)],
                    other.at[pl.ds(there, count)],
                    send_sem.at[n],
                    recv_sem.at[n],
                    side,
                ),
            )
        )
    for away in range(1, HALO + 1):
        for k, dx in enumerate((-1, 1)):
            if dx == -1:
                source, target = HALO + away - 1, HALO + cells_x + away - 1
            else:
                source, target = HALO + cells_x - away, HALO - away
            fields = pl.ds(0, SENT)
            if away == HALO:
                fields = pl.ds(0 if dx == 1 else RHS_HIGH, OUTER)
            rowwise[dx, away] = remote(
                sent.at[source, fields],
                sent.at[target, fields],
                row_send_sem.at[k, away - 1],
                row_recv_sem.at[k, away - 1],
                (dx, 0),
            )
    def fields_at(dx, away):
        return pl.ds(0, SENT) if away < HALO else pl.ds(0 if dx == 1 else RHS_HIGH, OUTER)

    forwards = {1: [], -1: []}
    for away in range(DIRECT + 1, HALO + 1):
        for k, dx in enumerate((-1, 1)):
            if dx == 1:
                source, target, to = HALO + 2 * cells_x - away, HALO - away, 0
            else:
                source, target, to = HALO - cells_x + away - 1, HALO + cells_x + away - 1, last
            copy = pltpu.make_async_remote_copy(
                src_ref=sent.at[source, fields_at(dx, away)],
                dst_ref=sent.at[target, fields_at(dx, away)],
                send_sem=forward_sem.at[k, away - DIRECT - 1],
                recv_sem=row_recv_sem.at[k, away - 1],
                device_id=(to, me_y),
                device_id_type=pl.DeviceIdType.MESH,
            )
            forwards[dx].append((cells_x + 1 - away, copy))
    forwarder = {1: me_x == last - 1, -1: me_x == 1}

    copies = [(side, copy, True) for side, copy in small]
    first_rows = [cells_x + 1 - away for away in range(DIRECT + 1, HALO + 1)]
    at_end = {1: me_x == last, -1: me_x == 0}
    for dx in (-1, 1):
        for away in first_rows:
            copies.append(((dx, 0), rowwise[dx, away], at_end[-dx]))
    for (dx, away), copy in rowwise.items():
        sends = True
        if away in first_rows:
            sends = jnp.logical_not(at_end[-dx])
        if away > DIRECT:
            sends = sends & jnp.logical_not(at_end[dx])
        copies.append(((dx, 0), copy, sends))

    later = {side: by for side, by in zip(SIDES, waiting)}
    for side, copy, sends in copies:
        pl.when(jnp.logical_not(later[side]) & sends)(copy.start)
    for k in (0, 1):
        mine = {side: over(side)[k] & later[side] for side in SIDES}
        tokens = number(mine.values())
        tokens = jnp.where(at_corner, 1, tokens) if k == 0 else jnp.minimum(tokens, 1)

        @pl.when(tokens > 0)
        def _(mine=mine, tokens=tokens, k=k):
            pl.semaphore_wait(token.at[k], tokens)
            for side, copy, sends in copies:
                pl.when(mine[side] & sends)(copy.start)

    def forward(dx):
        for away, copy in forwards[dx]:
            rowwise[-dx, away].wait_recv()
            copy.start()

    pl.when(forwarder[1])(lambda: forward(1))

    def forward_back():
        pl.semaphore_wait(token.at[2], 1)
        forward(-1)

    theta = (LMAX + LMIN) / 2.0
    delta = (LMAX - LMIN) / 2.0
    s_one = theta / delta

    EVERY = range(SENT)
    main, strip = slice(0, cells_y), slice(cells_y, cells_y + LANES)

    def begin(row, at, right):
        residue[row, :, at] = right
        direction[0, row, :, at] = right * (1.0 / theta)
        pressure[row, :, at] = right * (1.0 / theta)

    def take(row, at, field, wanted):
        total = field(SIGMA) if len(wanted) == SENT else None
        for n in wanted:
            i = ORDER[n]
            if i >= 0:
                value = field(n)
                if total is not None:
                    total = total + value
                if OFFSETS[i][0] != 0:
                    value = jnp.where(leaves(OFFSETS[i][0], value.shape), 0.0, value)
                terms[row, n, :, at] = value
        if total is not None:
            diag[row, :, at] = total
        begin(row, at, field(RHS_HIGH) + field(RHS_LOW))

    def fields_of(row):
        if row == 0:
            return range(OUTER)
        return range(RHS_HIGH, RHS_HIGH + OUTER) if row == rows - 1 else EVERY

    EDGE, MIDDLE = 2 * HALO, LANES // 2

    def own_ends(row, field):
        for n in fields_of(row):
            low, high = field(n, 0), field(n, tiles - 1)
            ends[row, n] = jnp.where(
                lane < MIDDLE, roll(high, EDGE, 1), roll(low, MIDDLE + HALO, 1)
            )

    def take_strip(row):
        above = from_high[row].astype(jnp.float32)
        below = from_low[row].astype(jnp.float32)
        is_above = (lane >= EDGE) & (lane < EDGE + HALO)
        is_below = (lane >= MIDDLE) & (lane < MIDDLE + HALO)

        def field(n):
            value = jnp.where(is_above, roll(above, EDGE - HALO * n, 1), ends[row, n])
            return jnp.where(is_below, roll(below, MIDDLE - HALO * n, 1), value)

        take(row, strip, field, fields_of(row))

    def take_main(row, field):
        take(
            row,
            main,
            lambda n: jnp.concatenate([field(n, t) for t in range(tiles)], axis=1),
            fields_of(row),
        )
        own_ends(row, field)

    for x in range(cells_x):
        take_main(HALO + x, lambda n, t: turn[n, t, pl.ds(x, levels, stride=cells_x), :])

    factors = []
    rho = 1.0 / s_one
    for sweep in range(APPLIES):
        rho_new = 1.0 / (2.0 * s_one - rho)
        factors.append((rho_new * rho, 2.0 * rho_new / delta))
        rho = rho_new

    def apply(sweep, row, at):
        field = {k: direction[sweep - 1, row + k, :, at] for k in (-1, 0, 1)}

        def along(step_z, step_y):
            total = None
            for step_x in (-1, 0, 1):
                n = PLACE.get((step_z, step_x, step_y))
                if n is not None:
                    term = terms[row - step_x, n, :, at] * field[-step_x]
                    total = term if total is None else total + term
            return total

        def levels_moved(step_y):
            return roll(along(1, step_y), 1, 0) + roll(along(-1, step_y), -1, 0)

        total = along(0, 0) + levels_moved(0)
        total = total + roll(along(0, 1) + levels_moved(1), 1, 1)
        total = total + roll(along(0, -1) + levels_moved(-1), -1, 1)
        left = residue[row, :, at] - (diag[row, :, at] * field[0] - total)
        keep, add = factors[sweep - 1]
        value = keep * field[0] + add * left
        return row, at, left, value, pressure[row, :, at] + value

    def apply_rows(sweep, which, lanes):
        done = [apply(sweep, row, at) for row in which for at in lanes]
        for row, at, left, value, summed in done:
            residue[row, :, at] = left
            direction[sweep, row, :, at] = value
            pressure[row, :, at] = summed

    def wave(away, lanes):
        low, high = HALO - away, HALO + cells_x - 1 + away
        for sweep in range(1, APPLIES + 1):
            first, last_row = low + sweep, high - sweep
            if first < last_row:
                if away == 0:
                    for row in range(first, last_row, 2):
                        apply_rows(sweep, (row, row + 1), lanes)
                else:
                    apply_rows(sweep, (first, last_row), lanes)

    def rows_of(away):
        return ((1, HALO - away), (-1, HALO + cells_x - 1 + away))

    def receive_rows(away):
        for dx, row in rows_of(away):
            if away in first_rows:
                pl.when(jnp.logical_not(forwarder[-dx]))(rowwise[dx, away].wait_recv)
            else:
                rowwise[dx, away].wait_recv()
            take_main(row, lambda n, t: sent[row, n, :, spread(t)].astype(jnp.float32))

    pl.when(forwarder[-1])(forward_back)

    far = at_y_seam(me_y) & (me_x != 0) & (me_x != last)

    @pl.when(jnp.logical_not(far))
    def _():
        for _, copy in small:
            copy.wait_recv()
        for x in range(cells_x):
            take_strip(HALO + x)
        wave(0, (main, strip))
        for away in range(1, HALO + 1):
            receive_rows(away)
            for _, row in rows_of(away):
                take_strip(row)
            wave(away, (main, strip))

    @pl.when(far)
    def _():
        wave(0, (main,))
        for away in range(1, HALO + 1):
            receive_rows(away)
            wave(away, (main,))
        for _, copy in small:
            copy.wait_recv()
        for row in range(rows):
            take_strip(row)
        for sweep in range(1, APPLIES + 1):
            for row in range(sweep, rows - sweep, 2):
                apply_rows(sweep, (row, row + 1), (strip,))

    for n in range(cells_x + 2):
        row = HALO - 1 + n
        at_ends = pressure[row, :, strip]
        low, high = pressure[row, :, :LANES], pressure[row, :, cells_y - LANES : cells_y]
        low = jnp.where(lane < HALO, roll(at_ends, -MIDDLE - HALO, 1), low)
        high = jnp.where(lane >= LANES - HALO, roll(at_ends, -EDGE, 1), high)
        beyond = jnp.where(
            lane < MIDDLE, roll(at_ends, -EDGE, 1), roll(at_ends, LANES - MIDDLE - HALO, 1)
        )
        pressure_ref[n, :, :cells_y] = pressure[row, :, :cells_y]
        pressure_ref[n, :, :LANES] = low
        pressure_ref[n, :, cells_y - LANES : cells_y] = high
        pressure_ref[n, :, cells_y:] = beyond

    for _, copy, sends in copies:
        (copy.wait_send() if sends is True else pl.when(sends)(copy.wait_send))
    for dx in (1, -1):
        for _, copy in forwards[dx]:
            pl.when(forwarder[dx])(copy.wait_send)


def leaves(step_z, shape):
    level = lax.broadcasted_iota(jnp.int32, shape, 0)
    return level == (shape[0] - 1 if step_z == 1 else 0)


def correct(pressure, vel_ref, metric_ref, pressure_ref, out_ref, turn):
    levels, cells_x, cells_y = pressure_ref.shape
    tiles = cells_y // LANES
    shape = pressure.shape[1:]
    for x in range(cells_x):
        here = pressure[x + 1]
        grad_x = (pressure[x + 2] - pressure[x]) * 0.5
        grad_y = (roll(here, -1, 1) - roll(here, 1, 1)) * 0.5
        upper = jnp.where(leaves(1, shape), 0.0, roll(here, -1, 0))
        lower = jnp.where(leaves(-1, shape), 0.0, roll(here, 1, 0))
        grad_z = (upper - lower) * 0.5
        for n, value in enumerate((grad_x, grad_y, grad_z, here)):
            for t in range(tiles):
                turn[n, t, pl.ds(x * levels, levels), :] = value[:, t * LANES : (t + 1) * LANES]
    for z in range(levels):
        for t in range(tiles):
            at = slice(t * LANES, (t + 1) * LANES)
            back = [turn[n, t, pl.ds(z, cells_x, stride=levels), :] for n in range(4)]
            pressure_ref[z, :, at] = back[3]
            for n in range(3):
                out_ref[n, z, :, at] = (
                    vel_ref[n, z, :, at].astype(jnp.float32)
                    - metric_ref[n, z, :, at].astype(jnp.float32) * back[n]
                )


def on_device(count_x, count_y, coeffs, sigma, rhs, vel_bar, metric):
    levels, cells_x, cells_y = rhs.shape
    rows, width = cells_x + 2 * HALO, cells_y + LANES
    vmem = pl.BlockSpec(memory_space=pltpu.VMEM)
    hbm = pl.BlockSpec(memory_space=pltpu.HBM)
    pressure = pl.pallas_call(
        functools.partial(kernel, count_x, count_y),
        out_shape=jax.ShapeDtypeStruct((cells_x + 2, levels, width), jnp.float32),
        in_specs=[hbm] * 3,
        out_specs=vmem,
        scratch_shapes=[
            pltpu.VMEM(coeffs.shape, jnp.bfloat16),
            pltpu.VMEM(sigma.shape, jnp.float32),
            pltpu.VMEM(rhs.shape, jnp.float32),
            pltpu.SemaphoreType.DMA((3,)),
            pltpu.VMEM((rows, SENT, levels, cells_y), jnp.bfloat16),
            pltpu.VMEM((cells_x, levels, LANES), jnp.bfloat16),
            pltpu.VMEM((cells_x, levels, LANES), jnp.bfloat16),
            pltpu.VMEM((rows, levels, LANES), jnp.bfloat16),
            pltpu.VMEM((rows, levels, LANES), jnp.bfloat16),
            pltpu.VMEM((rows, SENT, levels, width), jnp.float32),
            pltpu.VMEM((rows, SENT, levels, LANES), jnp.float32),
            pltpu.VMEM((rows, levels, width), jnp.float32),
            pltpu.VMEM((SENT, cells_y // LANES, levels * cells_x, LANES), jnp.float32),
            pltpu.VMEM((SWEEPS, rows, levels, width), jnp.float32),
            pltpu.VMEM((rows, levels, width), jnp.float32),
            pltpu.VMEM((rows, levels, width), jnp.float32),
            pltpu.SemaphoreType.DMA((len(SIDES),)),
            pltpu.SemaphoreType.DMA((len(SIDES),)),
            pltpu.SemaphoreType.DMA((2, HALO)),
            pltpu.SemaphoreType.DMA((2, HALO)),
            pltpu.SemaphoreType.DMA((2, HALO - DIRECT)),
            pltpu.SemaphoreType.REGULAR((3,)),
        ],
        compiler_params=pltpu.CompilerParams(
            collective_id=0, has_side_effects=True, vmem_limit_bytes=32 << 20
        ),
    )(*(pltpu.with_memory_space_constraint(v, pltpu.HBM) for v in (coeffs, sigma, rhs)))
    return pl.pallas_call(
        correct,
        out_shape=(
            jax.ShapeDtypeStruct(rhs.shape, jnp.float32),
            jax.ShapeDtypeStruct(vel_bar.shape, jnp.float32),
        ),
        in_specs=[vmem] * 3,
        out_specs=(vmem, vmem),
        scratch_shapes=[pltpu.VMEM((4, cells_y // LANES, levels * cells_x, LANES), jnp.float32)],
        compiler_params=pltpu.CompilerParams(vmem_limit_bytes=8 << 20),
    )(pressure, vel_bar, metric)


def solution(mesh):
    return jax.shard_map(
        functools.partial(on_device, mesh.shape["gx"], mesh.shape["gy"]),
        mesh=mesh,
        in_specs=(
            P(None, None, "gx", "gy"),
            P(None, "gx", "gy"),
            P(None, "gx", "gy"),
            P(None, None, "gx", "gy"),
            P(None, None, "gx", "gy"),
        ),
        out_specs=(P(None, "gx", "gy"), P(None, None, "gx", "gy")),
        check_vma=False,
    )
```
